32 devices in a mesh: grp: 4 (over x, core), dev: 8 (over z, y).
Axes of the slice: x: 2, y: 2, z: 4, core: 2. Of those that a mesh axis runs over, the one named last changes fastest.
Arguments:
- coefficients: float32 [2, 8, 64, 4096], P(None, None, None, ('grp', 'dev')), may hold values from -6 to 6
- spatial_root: int32 [64], replicated, may hold values from 0 to 1023
- frequency_root: int32 [64], replicated, may hold values from 0 to 255
Outputs:
- result: float32 [2, 8, 64, 4096], P(None, None, None, ('grp', 'dev'))
The draws below stay inside these ranges and needn't reach their ends.
All inputs are finite; a program needn't handle non-finite values.
Results may differ from the reference program's by a relative error of at most 0.002.
Values sent between devices are 32-bit elements; how exact they have to be, the bound alone decides.
A program may use at most 64 MiB of HBM per device.

```python
import math
import jax
import jax.numpy as jnp
from jax import lax

R = 64
S = 8
LEVELS = 12
PD = 128
NB = 64
PAIRS = 4096
N_DEV = 8


def touch_ends(array, own_key, smallest, high):
    place = [jax.random.randint(jax.random.fold_in(own_key, axis), (), 0, length) for axis, length in enumerate(array.shape)]
    longest = array.shape.index(max(array.shape))
    neighbour = place[:longest] + [(place[longest] + 1) % array.shape[longest]] + place[longest + 1:]
    return array.at[tuple(place)].set(smallest).at[tuple(neighbour)].set(high)


def block_levels(stream_key, shape, shards, smallest, top_value):
    factor_of, own = 1.0, jax.random.fold_in(stream_key, 6)
    for dim, blocks in shards:
        draws = jnp.exp(jax.random.uniform(jax.random.fold_in(own, dim), (blocks,), jnp.float32, smallest / len(shards), top_value / len(shards)))
        factor_of = factor_of * jnp.repeat(draws, shape[dim] // blocks).reshape([-1 if axis == dim else 1 for axis in range(len(shape))])
    return factor_of


def noise(stream_key, dims, deviation, bound, pieces=(), kind=jnp.bfloat16):
    level = block_levels(stream_key, dims, pieces, -0.22, 0.18) if pieces else 1.0
    entries = jax.random.normal(stream_key, dims, jnp.float32) * deviation * level
    return jnp.minimum(jnp.maximum(entries, -bound), bound).astype(kind)


def setup_inputs(seed: int = 0) -> dict:
    keys = jax.random.split(jax.random.key(seed), 4)
    coefficients = noise(keys[0], (2, S, R, PAIRS), 1.0, 6.0, ((3, 32),), jnp.float32)
    spatial_root = touch_ends(jax.random.randint(keys[1], (NB,), 0, 4 ** (LEVELS // 2 - 1)), jax.random.fold_in(keys[1], 1), 0, (4 ** (LEVELS // 2 - 1)) - 1).astype(jnp.int32)
    frequency_root = touch_ends(jax.random.randint(keys[2], (NB,), 0, 4 ** (LEVELS // 2 - 2)), jax.random.fold_in(keys[2], 1), 0, (4 ** (LEVELS // 2 - 2)) - 1).astype(jnp.int32)
    return {"coefficients": coefficients, "spatial_root": spatial_root, "frequency_root": frequency_root}


HIGHEST = lax.Precision.HIGHEST

def cheb_nodes():
    node_order = jnp.arange(8, dtype=jnp.float32)
    return 0.5 - 0.5 * jnp.cos(math.pi * (2.0 * node_order + 1.0) / 16.0)

def lagrange_table(half_cell):
    points = cheb_nodes()
    target = (points + half_cell) / 2.0
    diagonal = jnp.arange(8)[:, None] == jnp.arange(8)[None, :]
    numerator = jnp.where(diagonal[None, :, :], jnp.float32(1.0), target[:, None, None] - points[None, None, :])
    denominator = jnp.where(diagonal, jnp.float32(1.0), points[:, None] - points[None, :])
    return jnp.prod(numerator, axis=2) / jnp.prod(denominator, axis=1)[None, :]

def interp_tables():
    halves = [lagrange_table(0.0), lagrange_table(1.0)]
    return jnp.stack([jnp.kron(halves[quadrant % 2], halves[quadrant // 2]) for quadrant in range(4)])

def pair_digits(pair_index, pairs_dev, devices_dev):
    quarter = pairs_dev // 4
    within = pair_index % pairs_dev
    device = pair_index // pairs_dev % devices_dev
    group_id = pair_index // (pairs_dev * devices_dev)
    places = [device % 4, group_id % 4, within // quarter]
    return (places, device // 4 * quarter + within % quarter)

def pair_boxes(pair_index, level_step, box_roots, pairs_dev, devices_dev, levels):
    places, _ = pair_digits(pair_index, pairs_dev, devices_dev)
    coarse_space = levels // 2 - 1
    coarse_wave = levels // 2 - 2
    space_row = box_roots[0] // 2 ** coarse_space
    space_column = box_roots[0] % 2 ** coarse_space
    for position in range(level_step):
        space_row = 2 * space_row + places[position] % 2
        space_column = 2 * space_column + places[position] // 2
    wave_row = box_roots[1] // 2 ** coarse_wave
    wave_column = box_roots[1] % 2 ** coarse_wave
    for position in range(2, level_step - 1, -1):
        wave_row = 2 * wave_row + places[position] % 2
        wave_column = 2 * wave_column + places[position] // 2
    space_side = 0.5 ** (coarse_space + level_step)
    wave_side = float(2 ** levels) / float(2 ** (coarse_wave + 3 - level_step))
    offset = -0.5 * float(2 ** levels)
    space_box = (space_row.astype(jnp.float32) * space_side, space_column.astype(jnp.float32) * space_side, space_side)
    wave_box = (offset + wave_row.astype(jnp.float32) * wave_side, offset + wave_column.astype(jnp.float32) * wave_side, wave_side)
    return (space_box, wave_box)

def box_points(square):
    points = cheb_nodes()
    first_axis = jnp.repeat(points, 8)
    second_axis = jnp.tile(points, 8)
    return (square[0][None, :] + square[2] * first_axis[:, None], square[1][None, :] + square[2] * second_axis[:, None])

def box_center(square):
    return (square[0] + 0.5 * square[2], square[1] + 0.5 * square[2])

def phase_angle(first_space, second_space, first_wave, second_wave):
    two_pi = 2.0 * math.pi
    wave_speed = 16.0 * math.pi
    speed_one = (2.0 + jnp.sin(wave_speed * first_space) * jnp.sin(wave_speed * second_space)) / 16.0
    speed_two = (2.0 + jnp.cos(wave_speed * first_space) * jnp.cos(wave_speed * second_space)) / 16.0
    radial = jnp.sqrt(speed_one * speed_one * first_wave * first_wave + speed_two * speed_two * second_wave * second_wave)
    return two_pi * (first_space * first_wave + second_space * second_wave + radial)

def rotate(values, turn_angle):
    cosine = jnp.cos(turn_angle)
    sine_part = jnp.sin(turn_angle)
    return jnp.stack([values[0] * cosine - values[1] * sine_part, values[0] * sine_part + values[1] * cosine])

def pre_merge(children, new_index, new_roots, child_index, child_roots, pairs_dev, devices_dev, levels):
    space_box, wave_box = pair_boxes(new_index, 1, new_roots, pairs_dev, devices_dev, levels)
    center_one, center_two = box_center(space_box)
    turned = []
    for child_id in range(4):
        _, child_wave = pair_boxes(child_index[child_id], 0, (child_roots[0][child_id], child_roots[1][child_id]), pairs_dev, devices_dev, levels)
        wave_one, wave_two = box_points(child_wave)
        turned.append(rotate(children[child_id], -phase_angle(center_one[None, :], center_two[None, :], wave_one, wave_two)))
    summed = jnp.einsum('cst,caksm->aktm', interp_tables(), jnp.stack(turned), precision=HIGHEST)
    wave_one, wave_two = box_points(wave_box)
    return rotate(summed, phase_angle(center_one[None, :], center_two[None, :], wave_one, wave_two))

def switch_step(values, pair_index, box_roots, pairs_dev, devices_dev, levels):
    space_box, wave_box = pair_boxes(pair_index, 1, box_roots, pairs_dev, devices_dev, levels)
    space_one, space_two = box_points(space_box)
    wave_one, wave_two = box_points(wave_box)
    kernel_angle = phase_angle(space_one[:, None, :], space_two[:, None, :], wave_one[None, :, :], wave_two[None, :, :])
    cosine = jnp.cos(kernel_angle)
    sine_part = jnp.sin(kernel_angle)
    real_part = jnp.einsum('tsm,ksm->ktm', cosine, values[0], precision=HIGHEST) - jnp.einsum('tsm,ksm->ktm', sine_part, values[1], precision=HIGHEST)
    imag_part = jnp.einsum('tsm,ksm->ktm', sine_part, values[0], precision=HIGHEST) + jnp.einsum('tsm,ksm->ktm', cosine, values[1], precision=HIGHEST)
    return jnp.stack([real_part, imag_part]) / 64.0

def post_terms(values, pair_index, box_roots, level_step, pairs_dev, devices_dev, levels):
    space_box, wave_box = pair_boxes(pair_index, level_step, box_roots, pairs_dev, devices_dev, levels)
    space_one, space_two = box_points(space_box)
    center_one, center_two = box_center(wave_box)
    return rotate(values, -phase_angle(space_one, space_two, center_one[None, :], center_two[None, :]))

def post_finish(merged, pair_index, box_roots, level_step, pairs_dev, devices_dev, levels):
    space_box, wave_box = pair_boxes(pair_index, level_step, box_roots, pairs_dev, devices_dev, levels)
    space_one, space_two = box_points(space_box)
    center_one, center_two = box_center(wave_box)
    return rotate(merged, phase_angle(space_one, space_two, center_one[None, :], center_two[None, :]))

def lookup_roots(pair_index, spatial_root, frequency_root):
    _, block_id = pair_digits(pair_index, PD, N_DEV)
    return (jnp.take(spatial_root, block_id), jnp.take(frequency_root, block_id))

def reference(coefficients, spatial_root, frequency_root):
    rhs_count = coefficients.shape[1]
    rank_count = coefficients.shape[2]
    pairs = coefficients.shape[3]
    pair_index = jnp.arange(pairs, dtype=jnp.int32)
    box_roots = lookup_roots(pair_index, spatial_root, frequency_root)
    outer_count = pairs // (4 * PD)
    children = jnp.moveaxis(coefficients.reshape(2, rhs_count, rank_count, outer_count, 4, PD), 4, 0).reshape(4, 2, rhs_count, rank_count, outer_count * PD)
    child_index = jnp.moveaxis(pair_index.reshape(outer_count, 4, PD), 1, 0).reshape(4, outer_count * PD)
    child_roots = (jnp.moveaxis(box_roots[0].reshape(outer_count, 4, PD), 1, 0).reshape(4, outer_count * PD), jnp.moveaxis(box_roots[1].reshape(outer_count, 4, PD), 1, 0).reshape(4, outer_count * PD))
    merged = []
    for quadrant in range(4):
        outcome = pre_merge(children, child_index[quadrant], (child_roots[0][quadrant], child_roots[1][quadrant]), child_index, child_roots, PD, N_DEV, LEVELS)
        merged.append(outcome.reshape(2, rhs_count, rank_count, outer_count, PD))
    first_level = jnp.stack(merged, axis=4).reshape(2, rhs_count, rank_count, pairs)
    blocks = pairs // PD

    def switch_block(packed):
        return switch_step(packed[0], packed[1], (packed[2], packed[3]), PD, N_DEV, LEVELS)
    switched = lax.map(switch_block, (jnp.moveaxis(first_level.reshape(2, rhs_count, rank_count, blocks, PD), 3, 0), pair_index.reshape(blocks, PD), box_roots[0].reshape(blocks, PD), box_roots[1].reshape(blocks, PD)))
    switched = jnp.moveaxis(switched, 0, 3).reshape(2, rhs_count, rank_count, pairs)
    child_terms = post_terms(switched, pair_index, box_roots, 1, PD, N_DEV, LEVELS)
    summed = lax.optimization_barrier(jnp.sum(child_terms.reshape(2, rhs_count, rank_count, 4, pairs // 4), axis=3))
    spread = jnp.einsum('jts,aksm->aktjm', interp_tables(), summed, precision=HIGHEST).reshape(2, rhs_count, rank_count, pairs)
    second = post_finish(spread, pair_index, box_roots, 2, PD, N_DEV, LEVELS)
    child_terms = post_terms(second, pair_index, box_roots, 2, PD, N_DEV, LEVELS)
    summed = lax.optimization_barrier(jnp.sum(child_terms.reshape(2, rhs_count, rank_count, outer_count * 4, 4, PD // 4), axis=4))
    spread = jnp.einsum('jts,aksgm->aktgjm', interp_tables(), summed, precision=HIGHEST).reshape(2, rhs_count, rank_count, pairs)
    return post_finish(spread, pair_index, box_roots, 3, PD, N_DEV, LEVELS)
```

```python
import functools
import math

import jax
import jax.numpy as jnp
import ml_dtypes
import numpy as np
from jax import lax
from jax.experimental import pallas as pl
from jax.experimental.pallas import tpu as pltpu
from jax.sharding import PartitionSpec as P

LEVELS = 12
MESH = pl.DeviceIdType.MESH
LANES = 128
K_STEPS = 4
LAG_C = 3
LAG_E = 5

NODES = 0.5 - 0.5 * np.cos(np.pi * (2.0 * np.arange(8) + 1.0) / 16.0)


def lagrange(half):
    target = (NODES + half) / 2.0
    table = np.ones((8, 8))
    for s in range(8):
        for n in range(8):
            if n != s:
                table[:, s] *= (target - NODES[n]) / (NODES[s] - NODES[n])
    return table


HALVES = [lagrange(0.0), lagrange(1.0)]
INTERP = [np.kron(HALVES[u % 2], HALVES[u // 2]) for u in range(4)]


def split_table(matrix):
    wide = np.concatenate([matrix, matrix], axis=1)
    high = wide.astype(ml_dtypes.bfloat16)
    low = (wide - high.astype(np.float64)).astype(ml_dtypes.bfloat16)
    return np.concatenate([high, low], axis=0)


PRE_TABLE = np.stack(
    [split_table(np.concatenate([INTERP[u].T, INTERP[u ^ 1].T], axis=1)) for u in range(4)]
)
LAST_TABLE = np.stack(
    [split_table(np.concatenate([INTERP[j] @ INTERP[u] for j in range(4)], axis=1)) for u in range(4)]
)


def fit(function, degree):
    series = np.polynomial.chebyshev.Chebyshev.interpolate(function, degree, domain=[0.0, 0.2504])
    return series.convert(kind=np.polynomial.Polynomial, domain=[-1, 1], window=[-1, 1]).coef


def sine_over(g):
    f = np.sqrt(np.maximum(g, 1e-30))
    return np.sin(2 * np.pi * f) / f


COS_COEF = fit(lambda g: np.cos(2 * np.pi * np.sqrt(np.maximum(g, 0.0))), 6)
SIN_COEF = fit(sine_over, 6)


def horner(coef, g, scale):
    total = jnp.float32(coef[-1] * scale)
    for value in coef[-2::-1]:
        total = total * g + jnp.float32(value * scale)
    return total


def frac(turns):
    return turns - jnp.floor(turns + 0.5)


def cos_sin(turns, scale=1.0):
    f = frac(turns)
    g = f * f
    return horner(COS_COEF, g, scale), horner(SIN_COEF, g, scale) * f


def root_of(square):
    inverse = lax.rsqrt(square)
    first = square * inverse
    return first + (0.5 * inverse) * (square - first * first)


def speeds(x1, x2):
    cos1, sin1 = cos_sin(8.0 * x1)
    cos2, sin2 = cos_sin(8.0 * x2)
    one = (2.0 + sin1 * sin2) / 16.0
    two = (2.0 + cos1 * cos2) / 16.0
    return one * one, two * two


def turns_of(x1, x2, sq1, sq2, k1, k2):
    return (x1 * k1 + x2 * k2) + root_of(sq1 * (k1 * k1) + sq2 * (k2 * k2))


def flip(value, bit):
    return value + bit - 2 * bit * (value // bit % 2)


def split(values):
    high = values.astype(jnp.bfloat16)
    low = (values - high.astype(jnp.float32)).astype(jnp.bfloat16)
    return high, low


def kernel(
    space_ref, wave_ref, coef_hbm, pre_hbm, last_hbm, out_ref,
    own, from_y, to_z, from_z, part, packed, gathered,
    pre_tab, last_tab, rot_c, rot_s, ker_c, ker_s, pre_turn, fin_c, fin_s, spread,
    x_rows, x2k2, k_rows, rhs_pre, rhs_last,
    load_sem, ysend, yrecv, zsend, zrecv, gsend, grecv,
):
    rhs = coef_hbm.shape[1]
    grp = lax.axis_index("grp")
    dev = lax.axis_index("dev")
    u0 = dev % 4
    height = dev // 4
    dev_y = flip(dev, 1)
    dev_z = flip(dev, 2)
    peers = [flip(grp, 1), flip(grp, 2), flip(flip(grp, 1), 2)]

    barrier = pltpu.get_barrier_semaphore()
    for target in [(grp, dev_y), (grp, dev_z)] + [(peer, dev) for peer in peers]:
        pl.semaphore_signal(barrier, inc=1, device_id=target, device_id_type=MESH)
    loads = [
        pltpu.make_async_copy(coef_hbm, own, load_sem.at[0]),
        pltpu.make_async_copy(pre_hbm.at[u0], pre_tab, load_sem.at[1]),
        pltpu.make_async_copy(last_hbm.at[grp], last_tab, load_sem.at[2]),
    ]
    for load in loads:
        load.start()
    pl.semaphore_wait(barrier, 5)

    def y_copy(k):
        return pltpu.make_async_remote_copy(
            src_ref=coef_hbm.at[:, k], dst_ref=from_y.at[:, k], send_sem=ysend.at[k], recv_sem=yrecv.at[k],
            device_id=(grp, dev_y), device_id_type=MESH,
        )

    def z_copy(k):
        return pltpu.make_async_remote_copy(
            src_ref=to_z.at[k], dst_ref=from_z.at[k], send_sem=zsend.at[k], recv_sem=zrecv.at[k],
            device_id=(grp, dev_z), device_id_type=MESH,
        )

    def g_copy(k, which):
        return pltpu.make_async_remote_copy(
            src_ref=packed.at[k], dst_ref=gathered.at[which, k], send_sem=gsend.at[which, k],
            recv_sem=grecv.at[which, k], device_id=(peers[which], dev), device_id_type=MESH,
        )

    for k in range(rhs):
        y_copy(k).start()

    shape = (8, LANES)
    lane = lax.broadcasted_iota(jnp.int32, shape, 1)
    row = lax.broadcasted_iota(jnp.int32, shape, 0)
    quarter = LANES // 4
    u2 = lane // quarter
    place = lane % quarter
    space_root = jnp.zeros(shape, jnp.int32)
    wave_root = jnp.zeros(shape, jnp.int32)
    for r in range(quarter):
        space_root = jnp.where(place == r, space_ref[height * quarter + r], space_root)
        wave_root = jnp.where(place == r, wave_ref[height * quarter + r], wave_root)
    coarse_space = LEVELS // 2 - 1
    coarse_wave = LEVELS // 2 - 2
    places = [u0, grp % 4, u2]
    z_col = jnp.full(shape, float(NODES[0]), jnp.float32)
    for i in range(1, 8):
        z_col = jnp.where(row == i, jnp.float32(NODES[i]), z_col)

    def space_box(section, first):
        one = lax.shift_right_logical(space_root, jnp.int32(coarse_space))
        two = lax.bitwise_and(space_root, jnp.int32(2**coarse_space - 1))
        for position in range(section):
            digit = first if position == 0 else places[position]
            one = 2 * one + digit % 2
            two = 2 * two + digit // 2
        side = 0.5 ** (coarse_space + section)
        return one.astype(jnp.float32) * side, two.astype(jnp.float32) * side, side

    def wave_box(section, first):
        one = lax.shift_right_logical(wave_root, jnp.int32(coarse_wave))
        two = lax.bitwise_and(wave_root, jnp.int32(2**coarse_wave - 1))
        for position in range(2, section - 1, -1):
            digit = first if position == 0 else places[position]
            one = 2 * one + digit % 2
            two = 2 * two + digit // 2
        side = float(2**LEVELS) / float(2 ** (coarse_wave + 3 - section))
        start = -0.5 * float(2**LEVELS)
        return start + one.astype(jnp.float32) * side, start + two.astype(jnp.float32) * side, side

    def center(box):
        return box[0] + 0.5 * box[2], box[1] + 0.5 * box[2]

    def axis_points(box, i1):
        return box[0] + box[2] * float(NODES[i1]), box[1] + box[2] * z_col

    targets = [u0, flip(u0, 2)]
    children = [u0, flip(u0, 1)]
    for ti in range(2):
        a1, a2 = center(space_box(1, targets[ti]))
        sq1, sq2 = speeds(a1, a2)
        for ci in range(2):
            box = wave_box(0, children[ci])
            for i1 in range(8):
                k1, k2 = axis_points(box, i1)
                cosine, sine = cos_sin(turns_of(a1, a2, sq1, sq2, k1, k2))
                rot_c[ti, ci, pl.ds(8 * i1, 8), :] = cosine
                rot_s[ti, ci, pl.ds(8 * i1, 8), :] = sine
        if ti == 0:
            box = wave_box(1, u0)
            for i1 in range(8):
                k1, k2 = axis_points(box, i1)
                pre_turn[pl.ds(8 * i1, 8), :] = frac(turns_of(a1, a2, sq1, sq2, k1, k2))
    space_1 = space_box(1, u0)
    wave_1 = wave_box(1, u0)
    b1, b2 = center(wave_1)
    space_3 = space_box(3, u0)
    d1, d2 = center(wave_box(3, u0))
    for i1 in range(8):
        x1, x2 = axis_points(space_1, i1)
        sq1, sq2 = speeds(x1, x2)
        x_rows[0, i1] = x1
        x_rows[1, i1] = sq1
        x_rows[2, i1] = sq2
        x_rows[3, i1] = frac(turns_of(x1, x2, sq1, sq2, b1, b2))
        k2 = wave_1[1] + wave_1[2] * float(NODES[i1])
        k1 = wave_1[0] + wave_1[2] * float(NODES[i1])
        x2k2[i1] = x2 * k2
        k_rows[0, i1] = k1
        k_rows[1, i1] = k2 * k2
        x1, x2 = axis_points(space_3, i1)
        sq1, sq2 = speeds(x1, x2)
        cosine, sine = cos_sin(turns_of(x1, x2, sq1, sq2, d1, d2))
        fin_c[pl.ds(8 * i1, 8), :] = cosine
        fin_s[pl.ds(8 * i1, 8), :] = sine

    def kernel_rows(tb):
        x1 = x_rows[0, tb]
        sq1 = x_rows[1, tb]
        sq2 = x_rows[2, tb]
        turn = x_rows[3, tb]
        second = [sq2 * k_rows[1, s2] for s2 in range(8)]
        for s1 in range(8):
            k1 = k_rows[0, s1]
            first = sq1 * (k1 * k1)
            line = x1 * k1
            for s2 in range(8):
                s = 8 * s1 + s2
                angle = (line + x2k2[s2]) + root_of(first + second[s2])
                extra = jnp.broadcast_to(pre_turn[pl.ds(s, 1), :], shape) - turn
                cosine, sine = cos_sin(frac(angle) + extra, 1.0 / 64.0)
                ker_c[tb, s] = cosine
                ker_s[tb, s] = sine

    def stage_b(k):
        copy = y_copy(k)
        copy.wait_recv()
        for ci in range(2):
            held = own if ci == 0 else from_y
            real, imag = held[0, k], held[1, k]
            for ti in range(2):
                cosine, sine = rot_c[ti, ci], rot_s[ti, ci]
                for a, value in enumerate([real * cosine + imag * sine, imag * cosine - real * sine]):
                    high, low = split(value)
                    columns = pl.ds((2 * ti + a) * LANES, LANES)
                    rhs_pre[pl.ds(64 * ci, 64), columns] = high
                    rhs_pre[pl.ds(128 + 64 * ci, 64), columns] = low
        for ti in (1, 0):
            product = jnp.dot(
                pre_tab[...], rhs_pre[:, 2 * ti * LANES : (2 * ti + 2) * LANES],
                preferred_element_type=jnp.float32,
            )
            total = product[:64] + product[64:]
            place_of = to_z if ti == 1 else part
            place_of[k, 0] = total[:, :LANES]
            place_of[k, 1] = total[:, LANES:]
            if ti == 1:
                z_copy(k).start()

    group_16 = lax.broadcasted_iota(jnp.int32, (16, LANES), 1) // quarter

    def stage_c(k):
        z_copy(k).wait_recv()
        spread[...] = part[k] + from_z[k]

        def body(outer, sums):
            sums = list(sums)
            for inner in range(8):
                s = 8 * outer + inner
                real = jnp.broadcast_to(spread[0, pl.ds(s, 1), :], shape)
                imag = jnp.broadcast_to(spread[1, pl.ds(s, 1), :], shape)
                for tb in range(8):
                    cosine, sine = ker_c[tb, s], ker_s[tb, s]
                    sums[2 * tb] += cosine * real - sine * imag
                    sums[2 * tb + 1] += sine * real + cosine * imag
            return tuple(sums)

        sums = lax.fori_loop(0, 8, body, tuple(jnp.zeros(shape, jnp.float32) for _ in range(16)))
        for a in range(2):
            sets = [jnp.concatenate([sums[4 * g + a], sums[4 * g + 2 + a]], axis=0) for g in range(4)]
            total = None
            for d in range(4):
                chosen = sets[(3 - d) % 4]
                for g in range(3):
                    chosen = jnp.where(group_16 == g, sets[(g - d) % 4], chosen)
                if d:
                    chosen = pltpu.roll(chosen, LANES - quarter * d, 1)
                total = chosen if total is None else total + chosen
            packed[k, a] = total
        for which in range(3):
            g_copy(k, which).start()

    def stage_e(k):
        for which in range(3):
            g_copy(k, which).wait_recv()
        for a in range(2):
            total = (packed[k, a] + gathered[0, k, a]) + (gathered[1, k, a] + gathered[2, k, a])
            high = total.astype(jnp.bfloat16).astype(jnp.float32)
            for level, value in enumerate([high, total - high]):
                rolled = [value] + [pltpu.roll(value, quarter * d, 1) for d in range(1, 4)]
                for j in range(4):
                    for g in range(4):
                        rows = pl.ds(256 * level + 64 * j + 16 * g, 16)
                        rhs_last[rows, pl.ds(a * LANES, LANES)] = jnp.where(
                            group_16 == j, rolled[(j - g) % 4], 0.0
                        ).astype(jnp.bfloat16)
        product = jnp.dot(last_tab[...], rhs_last[...], preferred_element_type=jnp.float32)
        total = product[:64] + product[64:]
        real, imag = total[:, :LANES], total[:, LANES:]
        cosine, sine = fin_c[...], fin_s[...]
        out_ref[0, k] = real * cosine - imag * sine
        out_ref[1, k] = real * sine + imag * cosine

    for load in loads:
        load.wait()

    per_step = 8 // K_STEPS

    def step(i, carry):
        @pl.when(i < K_STEPS)
        def _():
            def rows(j, inner):
                kernel_rows(i * per_step + j)
                return inner

            lax.fori_loop(0, per_step, rows, 0)

        @pl.when(i < rhs)
        def _():
            stage_b(i)

        @pl.when(jnp.logical_and(i >= LAG_C, i < LAG_C + rhs))
        def _():
            stage_c(i - LAG_C)

        @pl.when(i >= LAG_E)
        def _():
            stage_e(i - LAG_E)

        return carry

    lax.fori_loop(0, rhs + LAG_E, step, 0)
    for k in range(rhs):
        y_copy(k).wait_send()
        z_copy(k).wait_send()
        for which in range(3):
            g_copy(k, which).wait_send()


def per_device(coefficients, spatial_root, frequency_root):
    _, rhs, rank, pairs = coefficients.shape
    block = (2, rhs, rank, pairs)
    f32 = jnp.float32
    hbm = pl.BlockSpec(memory_space=pl.ANY)
    smem = pl.BlockSpec(memory_space=pltpu.SMEM)
    vmem = pl.BlockSpec(memory_space=pltpu.VMEM)
    tile = (8, LANES)
    table = (rank, LANES)
    dma = pltpu.SemaphoreType.DMA
    return pl.pallas_call(
        kernel,
        name="butterfly",
        out_shape=jax.ShapeDtypeStruct(block, f32),
        in_specs=[smem, smem, hbm, hbm, hbm],
        out_specs=vmem,
        scratch_shapes=[
            pltpu.VMEM(block, f32),
            pltpu.VMEM(block, f32),
            pltpu.VMEM((rhs, 2) + table, f32),
            pltpu.VMEM((rhs, 2) + table, f32),
            pltpu.VMEM((rhs, 2) + table, f32),
            pltpu.VMEM((rhs, 2, 16, LANES), f32),
            pltpu.VMEM((3, rhs, 2, 16, LANES), f32),
            pltpu.VMEM(PRE_TABLE.shape[1:], jnp.bfloat16),
            pltpu.VMEM(LAST_TABLE.shape[1:], jnp.bfloat16),
            pltpu.VMEM((2, 2) + table, f32),
            pltpu.VMEM((2, 2) + table, f32),
            pltpu.VMEM((8, rank) + tile, f32),
            pltpu.VMEM((8, rank) + tile, f32),
            pltpu.VMEM(table, f32),
            pltpu.VMEM(table, f32),
            pltpu.VMEM(table, f32),
            pltpu.VMEM((2,) + table, f32),
            pltpu.VMEM((4, 8) + tile, f32),
            pltpu.VMEM((8,) + tile, f32),
            pltpu.VMEM((2, 8) + tile, f32),
            pltpu.VMEM((256, 4 * LANES), jnp.bfloat16),
            pltpu.VMEM((512, 2 * LANES), jnp.bfloat16),
            dma((3,)),
            dma((rhs,)),
            dma((rhs,)),
            dma((rhs,)),
            dma((rhs,)),
            dma((3, rhs)),
            dma((3, rhs)),
        ],
        compiler_params=pltpu.CompilerParams(
            collective_id=0, has_side_effects=True, vmem_limit_bytes=32 * 2**20
        ),
    )(spatial_root, frequency_root, coefficients, jnp.asarray(PRE_TABLE), jnp.asarray(LAST_TABLE))


def solution(mesh):
    return jax.shard_map(
        per_device,
        mesh=mesh,
        in_specs=(P(None, None, None, ("grp", "dev")), P(), P()),
        out_specs=P(None, None, None, ("grp", "dev")),
        check_vma=False,
    )
```

```python
import functools
import math

import jax
import jax.numpy as jnp
import ml_dtypes
import numpy as np
from jax import lax
from jax.experimental import pallas as pl
from jax.experimental.pallas import tpu as pltpu
from jax.sharding import PartitionSpec as P

LEVELS = 12
MESH = pl.DeviceIdType.MESH
LANES = 128
K_PLAN = (2, 3, 3)
AHEAD = 3
LAG_C = 2
LAG_E = 4
UNROLL = 8

NODES = 0.5 - 0.5 * np.cos(np.pi * (2.0 * np.arange(8) + 1.0) / 16.0)


def lagrange(half):
    target = (NODES + half) / 2.0
    table = np.ones((8, 8))
    for s in range(8):
        for n in range(8):
            if n != s:
                table[:, s] *= (target - NODES[n]) / (NODES[s] - NODES[n])
    return table


HALVES = [lagrange(0.0), lagrange(1.0)]
INTERP = [np.kron(HALVES[u % 2], HALVES[u // 2]) for u in range(4)]


def split_table(matrix):
    wide = np.concatenate([matrix, matrix], axis=1)
    high = wide.astype(ml_dtypes.bfloat16)
    low = (wide - high.astype(np.float64)).astype(ml_dtypes.bfloat16)
    return np.concatenate([high, low], axis=0)


PRE_TABLE = np.stack(
    [
        np.stack([split_table(np.concatenate([INTERP[u].T, INTERP[u ^ bit].T], axis=1)) for bit in (1, 2)])
        for u in range(4)
    ]
)
LAST_TABLE = np.stack(
    [split_table(np.concatenate([INTERP[j] @ INTERP[u] for j in range(4)], axis=1)) for u in range(4)]
)


def fit(function, degree):
    series = np.polynomial.chebyshev.Chebyshev.interpolate(function, degree, domain=[0.0, 0.2504])
    return series.convert(kind=np.polynomial.Polynomial, domain=[-1, 1], window=[-1, 1]).coef


def sine_over(g):
    f = np.sqrt(np.maximum(g, 1e-30))
    return np.sin(2 * np.pi * f) / f


COS_COEF = fit(lambda g: np.cos(2 * np.pi * np.sqrt(np.maximum(g, 0.0))), 6)
SIN_COEF = fit(sine_over, 6)


def horner(coef, g, scale):
    total = jnp.float32(coef[-1] * scale)
    for value in coef[-2::-1]:
        total = total * g + jnp.float32(value * scale)
    return total


def frac(turns):
    return turns - jnp.floor(turns + 0.5)


def cos_sin(turns, scale=1.0):
    f = frac(turns)
    g = f * f
    return horner(COS_COEF, g, scale), horner(SIN_COEF, g, scale) * f


def root_of(square):
    inverse = lax.rsqrt(square)
    first = square * inverse
    return first + (0.5 * inverse) * (square - first * first)


def speeds(x1, x2):
    cos1, sin1 = cos_sin(8.0 * x1)
    cos2, sin2 = cos_sin(8.0 * x2)
    one = (2.0 + sin1 * sin2) / 16.0
    two = (2.0 + cos1 * cos2) / 16.0
    return one * one, two * two


def turns_of(x1, x2, sq1, sq2, k1, k2):
    return (x1 * k1 + x2 * k2) + root_of(sq1 * (k1 * k1) + sq2 * (k2 * k2))


def flip(value, bit):
    return value + bit - 2 * bit * (value // bit % 2)


def split(values):
    high = values.astype(jnp.bfloat16)
    low = (values - high.astype(jnp.float32)).astype(jnp.bfloat16)
    return high, low


def kernel(
    space_hbm, wave_hbm, coef_hbm, pre_hbm, last_hbm, out_ref,
    own, from_first, to_second, from_second, part, packed, gathered,
    pre_tab, last_tab, rot_c, rot_s, ker, pre_turn, fin_c, fin_s, spread,
    x_rows, x2k2, k_rows, rhs_pre, rhs_last,
    space_ref, wave_ref, load_sem, fsend, frecv, ssend, srecv, gsend, grecv,
):
    rhs = coef_hbm.shape[1]
    grp = lax.axis_index("grp")
    dev = lax.axis_index("dev")
    u0 = dev % 4
    height = dev // 4
    dev_y = flip(dev, 1)
    dev_z = flip(dev, 2)
    peers = [flip(grp, 1), flip(grp, 2), flip(flip(grp, 1), 2)]

    barrier = pltpu.get_barrier_semaphore()
    for target in [(grp, dev_y), (grp, dev_z)] + [(peer, dev) for peer in peers]:
        pl.semaphore_signal(barrier, inc=1, device_id=target, device_id_type=MESH)
    roots = [
        pltpu.make_async_copy(space_hbm, space_ref, load_sem.at[3]),
        pltpu.make_async_copy(wave_hbm, wave_ref, load_sem.at[4]),
    ]
    loads = [
        pltpu.make_async_copy(coef_hbm, own, load_sem.at[0]),
        pltpu.make_async_copy(pre_hbm.at[u0], pre_tab, load_sem.at[1]),
        pltpu.make_async_copy(last_hbm.at[grp], last_tab, load_sem.at[2]),
    ]
    for load in roots + loads:
        load.start()
    pl.semaphore_wait(barrier, 5)

    across = [dev_y, dev_z]

    def first_copy(k):
        return pltpu.make_async_remote_copy(
            src_ref=coef_hbm.at[:, k], dst_ref=from_first.at[:, k], send_sem=fsend.at[k], recv_sem=frecv.at[k],
            device_id=(grp, across[k % 2]), device_id_type=MESH,
        )

    def second_copy(k):
        return pltpu.make_async_remote_copy(
            src_ref=to_second.at[k], dst_ref=from_second.at[k], send_sem=ssend.at[k], recv_sem=srecv.at[k],
            device_id=(grp, across[1 - k % 2]), device_id_type=MESH,
        )

    def g_copy(j, which):
        return pltpu.make_async_remote_copy(
            src_ref=packed.at[j], dst_ref=gathered.at[which, j], send_sem=gsend.at[which, j],
            recv_sem=grecv.at[which, j], device_id=(peers[which], dev), device_id_type=MESH,
        )

    for k in range(2 * AHEAD):
        first_copy(k).start()

    for root in roots:
        root.wait()

    shape = (8, LANES)
    lane = lax.broadcasted_iota(jnp.int32, shape, 1)
    row = lax.broadcasted_iota(jnp.int32, shape, 0)
    quarter = LANES // 4
    u2 = lane // quarter
    place = lane % quarter
    space_root = jnp.zeros(shape, jnp.int32)
    wave_root = jnp.zeros(shape, jnp.int32)
    for r in range(quarter):
        space_root = jnp.where(place == r, space_ref[height * quarter + r], space_root)
        wave_root = jnp.where(place == r, wave_ref[height * quarter + r], wave_root)
    coarse_space = LEVELS // 2 - 1
    coarse_wave = LEVELS // 2 - 2
    places = [u0, grp % 4, u2]
    z_col = jnp.full(shape, float(NODES[0]), jnp.float32)
    for i in range(1, 8):
        z_col = jnp.where(row == i, jnp.float32(NODES[i]), z_col)

    def space_box(section, first):
        one = lax.shift_right_logical(space_root, jnp.int32(coarse_space))
        two = lax.bitwise_and(space_root, jnp.int32(2**coarse_space - 1))
        for position in range(section):
            digit = first if position == 0 else places[position]
            one = 2 * one + digit % 2
            two = 2 * two + digit // 2
        side = 0.5 ** (coarse_space + section)
        return one.astype(jnp.float32) * side, two.astype(jnp.float32) * side, side

    def wave_box(section, first):
        one = lax.shift_right_logical(wave_root, jnp.int32(coarse_wave))
        two = lax.bitwise_and(wave_root, jnp.int32(2**coarse_wave - 1))
        for position in range(2, section - 1, -1):
            digit = first if position == 0 else places[position]
            one = 2 * one + digit % 2
            two = 2 * two + digit // 2
        side = float(2**LEVELS) / float(2 ** (coarse_wave + 3 - section))
        start = -0.5 * float(2**LEVELS)
        return start + one.astype(jnp.float32) * side, start + two.astype(jnp.float32) * side, side

    def center(box):
        return box[0] + 0.5 * box[2], box[1] + 0.5 * box[2]

    def axis_points(box, i1):
        return box[0] + box[2] * float(NODES[i1]), box[1] + box[2] * z_col

    near, far = flip(u0, 1), flip(u0, 2)
    plan = [(u0, [(0, u0), (1, near), (4, far)]), (far, [(2, u0), (3, near)]), (near, [(5, u0), (6, far)])]
    rotation = [[[0, 1], [2, 3]], [[0, 4], [5, 6]]]
    for ti, (target, children) in enumerate(plan):
        a1, a2 = center(space_box(1, target))
        sq1, sq2 = speeds(a1, a2)
        for ri, child in children:
            box = wave_box(0, child)
            for i1 in range(8):
                k1, k2 = axis_points(box, i1)
                cosine, sine = cos_sin(turns_of(a1, a2, sq1, sq2, k1, k2))
                rot_c[ri, pl.ds(8 * i1, 8), :] = cosine
                rot_s[ri, pl.ds(8 * i1, 8), :] = sine
        if ti == 0:
            box = wave_box(1, u0)
            for i1 in range(8):
                k1, k2 = axis_points(box, i1)
                pre_turn[pl.ds(8 * i1, 8), :] = frac(turns_of(a1, a2, sq1, sq2, k1, k2))
    space_1 = space_box(1, u0)
    wave_1 = wave_box(1, u0)
    b1, b2 = center(wave_1)
    space_3 = space_box(3, u0)
    d1, d2 = center(wave_box(3, u0))
    for i1 in range(8):
        x1, x2 = axis_points(space_1, i1)
        sq1, sq2 = speeds(x1, x2)
        x_rows[0, i1] = x1
        x_rows[1, i1] = sq1
        x_rows[2, i1] = sq2
        x_rows[3, i1] = frac(turns_of(x1, x2, sq1, sq2, b1, b2))
        k2 = wave_1[1] + wave_1[2] * float(NODES[i1])
        k1 = wave_1[0] + wave_1[2] * float(NODES[i1])
        x2k2[i1] = x2 * k2
        k_rows[0, i1] = k1
        k_rows[1, i1] = k2 * k2
        x1, x2 = axis_points(space_3, i1)
        sq1, sq2 = speeds(x1, x2)
        cosine, sine = cos_sin(turns_of(x1, x2, sq1, sq2, d1, d2))
        fin_c[pl.ds(8 * i1, 8), :] = cosine
        fin_s[pl.ds(8 * i1, 8), :] = sine

    def kernel_rows(tb):
        x1 = x_rows[0, tb]
        sq1 = x_rows[1, tb]
        sq2 = x_rows[2, tb]
        turn = x_rows[3, tb]
        second = [sq2 * k_rows[1, s2] for s2 in range(8)]
        for s1 in range(8):
            k1 = k_rows[0, s1]
            first = sq1 * (k1 * k1)
            line = x1 * k1
            for s2 in range(8):
                s = 8 * s1 + s2
                angle = (line + x2k2[s2]) + root_of(first + second[s2])
                extra = jnp.broadcast_to(pre_turn[pl.ds(s, 1), :], shape) - turn
                cosine, sine = cos_sin(frac(angle) + extra, 1.0 / 64.0)
                ker[0, tb, s] = cosine
                ker[1, tb, s] = sine - cosine
                ker[2, tb, s] = sine + cosine

    def stage_b(k):
        kind = k % 2
        first_copy(k).wait_recv()
        for ci in range(2):
            held = own if ci == 0 else from_first
            real, imag = held[0, k], held[1, k]
            for ti in range(2):
                ri = rotation[kind][ti][ci]
                cosine, sine = rot_c[ri], rot_s[ri]
                for a, value in enumerate([real * cosine + imag * sine, imag * cosine - real * sine]):
                    high, low = split(value)
                    columns = pl.ds((2 * ti + a) * LANES, LANES)
                    rhs_pre[kind, pl.ds(64 * ci, 64), columns] = high
                    rhs_pre[kind, pl.ds(128 + 64 * ci, 64), columns] = low
        for ti in (1, 0):
            product = jnp.dot(
                pre_tab[kind], rhs_pre[kind, :, 2 * ti * LANES : (2 * ti + 2) * LANES],
                preferred_element_type=jnp.float32,
            )
            total = product[:64] + product[64:]
            place_of = to_second if ti == 1 else part
            place_of[k, 0] = total[:, :LANES]
            place_of[k, 1] = total[:, LANES:]
            if ti == 1:
                second_copy(k).start()

    group_16 = lax.broadcasted_iota(jnp.int32, (16, LANES), 1) // quarter

    def stage_c(j):
        for e in range(2):
            k = 2 * j + e
            second_copy(k).wait_recv()
            real = part[k, 0] + from_second[k, 0]
            imag = part[k, 1] + from_second[k, 1]
            spread[e, 0] = real + imag
            spread[e, 1] = real
            spread[e, 2] = imag

        def body(outer, sums):
            sums = list(sums)
            for inner in range(UNROLL):
                s = UNROLL * outer + inner
                rows = [[jnp.broadcast_to(spread[e, q, pl.ds(s, 1), :], shape) for q in range(3)] for e in range(2)]
                for tb in range(8):
                    for q in range(3):
                        entry = ker[q, tb, s]
                        for e in range(2):
                            sums[24 * e + 3 * tb + q] += entry * rows[e][q]
            return tuple(sums)

        sums = lax.fori_loop(0, 64 // UNROLL, body, tuple(jnp.zeros(shape, jnp.float32) for _ in range(48)))
        for e in range(2):
            three = [sums[24 * e + 3 * tb : 24 * e + 3 * tb + 3] for tb in range(8)]
            for a, parts in enumerate([[p[0] - p[2] for p in three], [p[0] + p[1] for p in three]]):
                sets = [jnp.concatenate([parts[2 * g], parts[2 * g + 1]], axis=0) for g in range(4)]
                total = None
                for d in range(4):
                    chosen = sets[(3 - d) % 4]
                    for g in range(3):
                        chosen = jnp.where(group_16 == g, sets[(g - d) % 4], chosen)
                    if d:
                        chosen = pltpu.roll(chosen, LANES - quarter * d, 1)
                    total = chosen if total is None else total + chosen
                packed[j, e, a] = total
        for which in (2, 1, 0):
            g_copy(j, which).start()

    def stage_e(j):
        for which in range(3):
            g_copy(j, which).wait_recv()
        for e in range(2):
            for a in range(2):
                total = (packed[j, e, a] + gathered[0, j, e, a]) + (gathered[1, j, e, a] + gathered[2, j, e, a])
                high = total.astype(jnp.bfloat16).astype(jnp.float32)
                for level, value in enumerate([high, total - high]):
                    rolled = [value] + [pltpu.roll(value, quarter * d, 1) for d in range(1, 4)]
                    for jj in range(4):
                        for g in range(4):
                            rows = pl.ds(256 * level + 64 * jj + 16 * g, 16)
                            rhs_last[rows, pl.ds((2 * e + a) * LANES, LANES)] = jnp.where(
                                group_16 == jj, rolled[(jj - g) % 4], 0.0
                            ).astype(jnp.bfloat16)
        product = jnp.dot(last_tab[...], rhs_last[...], preferred_element_type=jnp.float32)
        total = product[:64] + product[64:]
        cosine, sine = fin_c[...], fin_s[...]
        for e in range(2):
            real = total[:, 2 * e * LANES : (2 * e + 1) * LANES]
            imag = total[:, (2 * e + 1) * LANES : (2 * e + 2) * LANES]
            out_ref[0, 2 * j + e] = real * cosine - imag * sine
            out_ref[1, 2 * j + e] = real * sine + imag * cosine

    k_ends = np.cumsum((0,) + K_PLAN)

    def kernel_part(part_id):
        def rows(tb, inner):
            kernel_rows(tb)
            return inner

        if part_id < len(K_PLAN):
            lax.fori_loop(int(k_ends[part_id]), int(k_ends[part_id + 1]), rows, 0)

    kernel_part(0)
    pairs = rhs // 2
    for load in loads:
        load.wait()
    for i in range(pairs + LAG_E):
        if i < pairs:
            for e in range(2):
                stage_b(2 * i + e)
            if i + AHEAD < pairs:
                for e in range(2):
                    first_copy(2 * (i + AHEAD) + e).start()
        kernel_part(i + 1)
        if 0 <= i - LAG_C < pairs:
            stage_c(i - LAG_C)
        if i >= LAG_E:
            stage_e(i - LAG_E)
    for k in range(rhs):
        first_copy(k).wait_send()
        second_copy(k).wait_send()
    for j in range(pairs):
        for which in range(3):
            g_copy(j, which).wait_send()


def per_device(coefficients, spatial_root, frequency_root):
    _, rhs, rank, pairs = coefficients.shape
    block = (2, rhs, rank, pairs)
    f32 = jnp.float32
    hbm = pl.BlockSpec(memory_space=pltpu.HBM)
    vmem = pl.BlockSpec(memory_space=pltpu.VMEM)
    tile = (8, LANES)
    table = (rank, LANES)
    dma = pltpu.SemaphoreType.DMA
    return pl.pallas_call(
        kernel,
        name="butterfly",
        out_shape=jax.ShapeDtypeStruct(block, f32),
        in_specs=[hbm] * 5,
        out_specs=vmem,
        scratch_shapes=[
            pltpu.VMEM(block, f32),
            pltpu.VMEM(block, f32),
            pltpu.VMEM((rhs, 2) + table, f32),
            pltpu.VMEM((rhs, 2) + table, f32),
            pltpu.VMEM((rhs, 2) + table, f32),
            pltpu.VMEM((rhs // 2, 2, 2, 16, LANES), f32),
            pltpu.VMEM((3, rhs // 2, 2, 2, 16, LANES), f32),
            pltpu.VMEM(PRE_TABLE.shape[1:], jnp.bfloat16),
            pltpu.VMEM(LAST_TABLE.shape[1:], jnp.bfloat16),
            pltpu.VMEM((7,) + table, f32),
            pltpu.VMEM((7,) + table, f32),
            pltpu.VMEM((3, 8, rank) + tile, f32),
            pltpu.VMEM(table, f32),
            pltpu.VMEM(table, f32),
            pltpu.VMEM(table, f32),
            pltpu.VMEM((2, 3) + table, f32),
            pltpu.VMEM((4, 8) + tile, f32),
            pltpu.VMEM((8,) + tile, f32),
            pltpu.VMEM((2, 8) + tile, f32),
            pltpu.VMEM((2, 256, 4 * LANES), jnp.bfloat16),
            pltpu.VMEM((512, 4 * LANES), jnp.bfloat16),
            pltpu.SMEM(spatial_root.shape, jnp.int32),
            pltpu.SMEM(frequency_root.shape, jnp.int32),
            dma((5,)),
            dma((rhs,)),
            dma((rhs,)),
            dma((rhs,)),
            dma((rhs,)),
            dma((3, rhs // 2)),
            dma((3, rhs // 2)),
        ],
        compiler_params=pltpu.CompilerParams(
            collective_id=0, has_side_effects=True, vmem_limit_bytes=60 * 2**20
        ),
    )(spatial_root, frequency_root, coefficients, jnp.asarray(PRE_TABLE), jnp.asarray(LAST_TABLE))


def solution(mesh):
    return jax.shard_map(
        per_device,
        mesh=mesh,
        in_specs=(P(None, None, None, ("grp", "dev")), P(), P()),
        out_specs=P(None, None, None, ("grp", "dev")),
        check_vma=False,
    )
```

```python
import functools
import math

import jax
import jax.numpy as jnp
import ml_dtypes
import numpy as np
from jax import lax
from jax.experimental import pallas as pl
from jax.experimental.pallas import tpu as pltpu
from jax.sharding import PartitionSpec as P

LEVELS = 12
MESH = pl.DeviceIdType.MESH
LANES = 128
K_PLAN = (2, 3, 3)
AHEAD = 3
LAG_C = 2
LAG_E = 4
UNROLL = 16

NODES = 0.5 - 0.5 * np.cos(np.pi * (2.0 * np.arange(8) + 1.0) / 16.0)


def lagrange(half):
    target = (NODES + half) / 2.0
    table = np.ones((8, 8))
    for s in range(8):
        for n in range(8):
            if n != s:
                table[:, s] *= (target - NODES[n]) / (NODES[s] - NODES[n])
    return table


HALVES = [lagrange(0.0), lagrange(1.0)]
INTERP = [np.kron(HALVES[u % 2], HALVES[u // 2]) for u in range(4)]


def split_table(matrix):
    wide = np.concatenate([matrix, matrix], axis=1)
    high = wide.astype(ml_dtypes.bfloat16)
    low = (wide - high.astype(np.float64)).astype(ml_dtypes.bfloat16)
    return np.concatenate([high, low], axis=0)


PRE_TABLE = np.stack(
    [
        np.stack([split_table(np.concatenate([INTERP[u].T, INTERP[u ^ bit].T], axis=1)) for bit in (1, 2)])
        for u in range(4)
    ]
)
LAST_TABLE = np.stack(
    [split_table(np.concatenate([INTERP[j] @ INTERP[u] for j in range(4)], axis=1)) for u in range(4)]
)


def fit(function, degree):
    series = np.polynomial.chebyshev.Chebyshev.interpolate(function, degree, domain=[0.0, 0.2504])
    return series.convert(kind=np.polynomial.Polynomial, domain=[-1, 1], window=[-1, 1]).coef


def sine_over(g):
    f = np.sqrt(np.maximum(g, 1e-30))
    return np.sin(2 * np.pi * f) / f


COS_COEF = fit(lambda g: np.cos(2 * np.pi * np.sqrt(np.maximum(g, 0.0))), 6)
SIN_COEF = fit(sine_over, 6)


def horner(coef, g, scale):
    total = jnp.float32(coef[-1] * scale)
    for value in coef[-2::-1]:
        total = total * g + jnp.float32(value * scale)
    return total


def frac(turns):
    return turns - jnp.floor(turns + 0.5)


def cos_sin(turns, scale=1.0):
    f = frac(turns)
    g = f * f
    return horner(COS_COEF, g, scale), horner(SIN_COEF, g, scale) * f


def root_of(square):
    inverse = lax.rsqrt(square)
    first = square * inverse
    return first + (0.5 * inverse) * (square - first * first)


def speeds(x1, x2):
    cos1, sin1 = cos_sin(8.0 * x1)
    cos2, sin2 = cos_sin(8.0 * x2)
    one = (2.0 + sin1 * sin2) / 16.0
    two = (2.0 + cos1 * cos2) / 16.0
    return one * one, two * two


def turns_of(x1, x2, sq1, sq2, k1, k2):
    return (x1 * k1 + x2 * k2) + root_of(sq1 * (k1 * k1) + sq2 * (k2 * k2))


def flip(value, bit):
    return value + bit - 2 * bit * (value // bit % 2)


def split(values):
    high = values.astype(jnp.bfloat16)
    low = (values - high.astype(jnp.float32)).astype(jnp.bfloat16)
    return high, low


def kernel(
    space_hbm, wave_hbm, coef_hbm, pre_hbm, last_hbm, out_ref,
    own, from_first, to_second, from_second, part, packed, gathered,
    pre_tab, last_tab, rot_c, rot_s, ker, pre_turn, fin_c, fin_s, spread,
    x_rows, x2k2, k_rows, rhs_pre, rhs_last,
    space_ref, wave_ref, load_sem, fsend, frecv, ssend, srecv, gsend, grecv,
):
    rhs = coef_hbm.shape[1]
    grp = lax.axis_index("grp")
    dev = lax.axis_index("dev")
    u0 = dev % 4
    height = dev // 4
    dev_y = flip(dev, 1)
    dev_z = flip(dev, 2)
    peers = [flip(grp, 1), flip(grp, 2), flip(flip(grp, 1), 2)]

    barrier = pltpu.get_barrier_semaphore()
    for target in [(grp, dev_y), (grp, dev_z)] + [(peer, dev) for peer in peers]:
        pl.semaphore_signal(barrier, inc=1, device_id=target, device_id_type=MESH)
    roots = [
        pltpu.make_async_copy(space_hbm, space_ref, load_sem.at[3]),
        pltpu.make_async_copy(wave_hbm, wave_ref, load_sem.at[4]),
    ]
    loads = [
        pltpu.make_async_copy(coef_hbm, own, load_sem.at[0]),
        pltpu.make_async_copy(pre_hbm.at[u0], pre_tab, load_sem.at[1]),
        pltpu.make_async_copy(last_hbm.at[grp], last_tab, load_sem.at[2]),
    ]
    for load in roots + loads:
        load.start()
    pl.semaphore_wait(barrier, 5)

    across = [dev_y, dev_z]

    def first_copy(k):
        return pltpu.make_async_remote_copy(
            src_ref=coef_hbm.at[:, k], dst_ref=from_first.at[:, k], send_sem=fsend.at[k], recv_sem=frecv.at[k],
            device_id=(grp, across[k % 2]), device_id_type=MESH,
        )

    def second_copy(k):
        return pltpu.make_async_remote_copy(
            src_ref=to_second.at[k], dst_ref=from_second.at[k], send_sem=ssend.at[k], recv_sem=srecv.at[k],
            device_id=(grp, across[1 - k % 2]), device_id_type=MESH,
        )

    def g_copy(j, which):
        return pltpu.make_async_remote_copy(
            src_ref=packed.at[j], dst_ref=gathered.at[which, j], send_sem=gsend.at[which, j],
            recv_sem=grecv.at[which, j], device_id=(peers[which], dev), device_id_type=MESH,
        )

    for k in range(2 * AHEAD):
        first_copy(k).start()

    for root in roots:
        root.wait()

    shape = (8, LANES)
    lane = lax.broadcasted_iota(jnp.int32, shape, 1)
    row = lax.broadcasted_iota(jnp.int32, shape, 0)
    quarter = LANES // 4
    u2 = lane // quarter
    place = lane % quarter
    space_root = jnp.zeros(shape, jnp.int32)
    wave_root = jnp.zeros(shape, jnp.int32)
    for r in range(quarter):
        space_root = jnp.where(place == r, space_ref[height * quarter + r], space_root)
        wave_root = jnp.where(place == r, wave_ref[height * quarter + r], wave_root)
    coarse_space = LEVELS // 2 - 1
    coarse_wave = LEVELS // 2 - 2
    places = [u0, grp % 4, u2]
    z_col = jnp.full(shape, float(NODES[0]), jnp.float32)
    for i in range(1, 8):
        z_col = jnp.where(row == i, jnp.float32(NODES[i]), z_col)

    def space_box(section, first):
        one = lax.shift_right_logical(space_root, jnp.int32(coarse_space))
        two = lax.bitwise_and(space_root, jnp.int32(2**coarse_space - 1))
        for position in range(section):
            digit = first if position == 0 else places[position]
            one = 2 * one + digit % 2
            two = 2 * two + digit // 2
        side = 0.5 ** (coarse_space + section)
        return one.astype(jnp.float32) * side, two.astype(jnp.float32) * side, side

    def wave_box(section, first):
        one = lax.shift_right_logical(wave_root, jnp.int32(coarse_wave))
        two = lax.bitwise_and(wave_root, jnp.int32(2**coarse_wave - 1))
        for position in range(2, section - 1, -1):
            digit = first if position == 0 else places[position]
            one = 2 * one + digit % 2
            two = 2 * two + digit // 2
        side = float(2**LEVELS) / float(2 ** (coarse_wave + 3 - section))
        start = -0.5 * float(2**LEVELS)
        return start + one.astype(jnp.float32) * side, start + two.astype(jnp.float32) * side, side

    def center(box):
        return box[0] + 0.5 * box[2], box[1] + 0.5 * box[2]

    def axis_points(box, i1):
        return box[0] + box[2] * float(NODES[i1]), box[1] + box[2] * z_col

    near, far = flip(u0, 1), flip(u0, 2)
    plan = [(u0, [(0, u0), (1, near), (4, far)]), (far, [(2, u0), (3, near)]), (near, [(5, u0), (6, far)])]
    rotation = [[[0, 1], [2, 3]], [[0, 4], [5, 6]]]
    for ti, (target, children) in enumerate(plan):
        a1, a2 = center(space_box(1, target))
        sq1, sq2 = speeds(a1, a2)
        for ri, child in children:
            box = wave_box(0, child)
            for i1 in range(8):
                k1, k2 = axis_points(box, i1)
                cosine, sine = cos_sin(turns_of(a1, a2, sq1, sq2, k1, k2))
                rot_c[ri, pl.ds(8 * i1, 8), :] = cosine
                rot_s[ri, pl.ds(8 * i1, 8), :] = sine
        if ti == 0:
            box = wave_box(1, u0)
            for i1 in range(8):
                k1, k2 = axis_points(box, i1)
                pre_turn[pl.ds(8 * i1, 8), :] = frac(turns_of(a1, a2, sq1, sq2, k1, k2))
    space_1 = space_box(1, u0)
    wave_1 = wave_box(1, u0)
    b1, b2 = center(wave_1)
    space_3 = space_box(3, u0)
    d1, d2 = center(wave_box(3, u0))
    for i1 in range(8):
        x1, x2 = axis_points(space_1, i1)
        sq1, sq2 = speeds(x1, x2)
        x_rows[0, i1] = x1
        x_rows[1, i1] = sq1
        x_rows[2, i1] = sq2
        x_rows[3, i1] = frac(turns_of(x1, x2, sq1, sq2, b1, b2))
        k2 = wave_1[1] + wave_1[2] * float(NODES[i1])
        k1 = wave_1[0] + wave_1[2] * float(NODES[i1])
        x2k2[i1] = x2 * k2
        k_rows[0, i1] = k1
        k_rows[1, i1] = k2 * k2
        x1, x2 = axis_points(space_3, i1)
        sq1, sq2 = speeds(x1, x2)
        cosine, sine = cos_sin(turns_of(x1, x2, sq1, sq2, d1, d2))
        fin_c[pl.ds(8 * i1, 8), :] = cosine
        fin_s[pl.ds(8 * i1, 8), :] = sine

    def kernel_rows(tb):
        x1 = x_rows[0, tb]
        sq1 = x_rows[1, tb]
        sq2 = x_rows[2, tb]
        turn = x_rows[3, tb]
        second = [sq2 * k_rows[1, s2] for s2 in range(8)]
        for s1 in range(8):
            k1 = k_rows[0, s1]
            first = sq1 * (k1 * k1)
            line = x1 * k1
            for s2 in range(8):
                s = 8 * s1 + s2
                angle = (line + x2k2[s2]) + root_of(first + second[s2])
                extra = jnp.broadcast_to(pre_turn[pl.ds(s, 1), :], shape) - turn
                cosine, sine = cos_sin(frac(angle) + extra, 1.0 / 64.0)
                ker[0, tb, s] = cosine
                ker[1, tb, s] = sine - cosine
                ker[2, tb, s] = sine + cosine

    def stage_b(k):
        kind = k % 2
        first_copy(k).wait_recv()
        for ci in range(2):
            held = own if ci == 0 else from_first
            real, imag = held[0, k], held[1, k]
            for ti in range(2):
                ri = rotation[kind][ti][ci]
                cosine, sine = rot_c[ri], rot_s[ri]
                for a, value in enumerate([real * cosine + imag * sine, imag * cosine - real * sine]):
                    high, low = split(value)
                    columns = pl.ds((2 * ti + a) * LANES, LANES)
                    rhs_pre[kind, pl.ds(64 * ci, 64), columns] = high
                    rhs_pre[kind, pl.ds(128 + 64 * ci, 64), columns] = low
        for ti in (1, 0):
            product = jnp.dot(
                pre_tab[kind], rhs_pre[kind, :, 2 * ti * LANES : (2 * ti + 2) * LANES],
                preferred_element_type=jnp.float32,
            )
            total = product[:64] + product[64:]
            place_of = to_second if ti == 1 else part
            place_of[k, 0] = total[:, :LANES]
            place_of[k, 1] = total[:, LANES:]
            if ti == 1:
                second_copy(k).start()

    group_16 = lax.broadcasted_iota(jnp.int32, (16, LANES), 1) // quarter

    def stage_c(j):
        for e in range(2):
            k = 2 * j + e
            second_copy(k).wait_recv()
            real = part[k, 0] + from_second[k, 0]
            imag = part[k, 1] + from_second[k, 1]
            spread[e, 0] = real + imag
            spread[e, 1] = real
            spread[e, 2] = imag

        def body(outer, sums):
            sums = list(sums)
            for inner in range(UNROLL):
                s = UNROLL * outer + inner
                rows = [[jnp.broadcast_to(spread[e, q, pl.ds(s, 1), :], shape) for q in range(3)] for e in range(2)]
                for tb in range(8):
                    for q in range(3):
                        entry = ker[q, tb, s]
                        for e in range(2):
                            sums[24 * e + 3 * tb + q] += entry * rows[e][q]
            return tuple(sums)

        sums = lax.fori_loop(0, 64 // UNROLL, body, tuple(jnp.zeros(shape, jnp.float32) for _ in range(48)))
        for e in range(2):
            three = [sums[24 * e + 3 * tb : 24 * e + 3 * tb + 3] for tb in range(8)]
            for a, parts in enumerate([[p[0] - p[2] for p in three], [p[0] + p[1] for p in three]]):
                sets = [jnp.concatenate([parts[2 * g], parts[2 * g + 1]], axis=0) for g in range(4)]
                total = None
                for d in range(4):
                    chosen = sets[(3 - d) % 4]
                    for g in range(3):
                        chosen = jnp.where(group_16 == g, sets[(g - d) % 4], chosen)
                    if d:
                        chosen = pltpu.roll(chosen, LANES - quarter * d, 1)
                    total = chosen if total is None else total + chosen
                packed[j, e, a] = total
        for which in (2, 1, 0):
            g_copy(j, which).start()

    def stage_e(j):
        for which in range(3):
            g_copy(j, which).wait_recv()
        for e in range(2):
            for a in range(2):
                total = (packed[j, e, a] + gathered[0, j, e, a]) + (gathered[1, j, e, a] + gathered[2, j, e, a])
                high = total.astype(jnp.bfloat16).astype(jnp.float32)
                for level, value in enumerate([high, total - high]):
                    rolled = [value] + [pltpu.roll(value, quarter * d, 1) for d in range(1, 4)]
                    for jj in range(4):
                        for g in range(4):
                            rows = pl.ds(256 * level + 64 * jj + 16 * g, 16)
                            rhs_last[rows, pl.ds((2 * e + a) * LANES, LANES)] = jnp.where(
                                group_16 == jj, rolled[(jj - g) % 4], 0.0
                            ).astype(jnp.bfloat16)
        product = jnp.dot(last_tab[...], rhs_last[...], preferred_element_type=jnp.float32)
        total = product[:64] + product[64:]
        cosine, sine = fin_c[...], fin_s[...]
        for e in range(2):
            real = total[:, 2 * e * LANES : (2 * e + 1) * LANES]
            imag = total[:, (2 * e + 1) * LANES : (2 * e + 2) * LANES]
            out_ref[0, 2 * j + e] = real * cosine - imag * sine
            out_ref[1, 2 * j + e] = real * sine + imag * cosine

    k_ends = np.cumsum((0,) + K_PLAN)

    def kernel_part(part_id):
        def rows(tb, inner):
            kernel_rows(tb)
            return inner

        if part_id < len(K_PLAN):
            lax.fori_loop(int(k_ends[part_id]), int(k_ends[part_id + 1]), rows, 0)

    kernel_part(0)
    pairs = rhs // 2
    for load in loads:
        load.wait()
    for i in range(pairs + LAG_E):
        if i < pairs:
            for e in range(2):
                stage_b(2 * i + e)
            if i + AHEAD < pairs:
                for e in range(2):
                    first_copy(2 * (i + AHEAD) + e).start()
        kernel_part(i + 1)
        if 0 <= i - LAG_C < pairs:
            stage_c(i - LAG_C)
        if i >= LAG_E:
            stage_e(i - LAG_E)
    for k in range(rhs):
        first_copy(k).wait_send()
        second_copy(k).wait_send()
    for j in range(pairs):
        for which in range(3):
            g_copy(j, which).wait_send()


def per_device(coefficients, spatial_root, frequency_root):
    _, rhs, rank, pairs = coefficients.shape
    block = (2, rhs, rank, pairs)
    f32 = jnp.float32
    hbm = pl.BlockSpec(memory_space=pltpu.HBM)
    vmem = pl.BlockSpec(memory_space=pltpu.VMEM)
    tile = (8, LANES)
    table = (rank, LANES)
    dma = pltpu.SemaphoreType.DMA
    operands = [spatial_root, frequency_root, coefficients, jnp.asarray(PRE_TABLE), jnp.asarray(LAST_TABLE)]
    return pl.pallas_call(
        kernel,
        name="butterfly",
        out_shape=jax.ShapeDtypeStruct(block, f32),
        in_specs=[hbm] * 5,
        out_specs=vmem,
        scratch_shapes=[
            pltpu.VMEM(block, f32),
            pltpu.VMEM(block, f32),
            pltpu.VMEM((rhs, 2) + table, f32),
            pltpu.VMEM((rhs, 2) + table, f32),
            pltpu.VMEM((rhs, 2) + table, f32),
            pltpu.VMEM((rhs // 2, 2, 2, 16, LANES), f32),
            pltpu.VMEM((3, rhs // 2, 2, 2, 16, LANES), f32),
            pltpu.VMEM(PRE_TABLE.shape[1:], jnp.bfloat16),
            pltpu.VMEM(LAST_TABLE.shape[1:], jnp.bfloat16),
            pltpu.VMEM((7,) + table, f32),
            pltpu.VMEM((7,) + table, f32),
            pltpu.VMEM((3, 8, rank) + tile, f32),
            pltpu.VMEM(table, f32),
            pltpu.VMEM(table, f32),
            pltpu.VMEM(table, f32),
            pltpu.VMEM((2, 3) + table, f32),
            pltpu.VMEM((4, 8) + tile, f32),
            pltpu.VMEM((8,) + tile, f32),
            pltpu.VMEM((2, 8) + tile, f32),
            pltpu.VMEM((2, 256, 4 * LANES), jnp.bfloat16),
            pltpu.VMEM((512, 4 * LANES), jnp.bfloat16),
            pltpu.SMEM(spatial_root.shape, jnp.int32),
            pltpu.SMEM(frequency_root.shape, jnp.int32),
            dma((5,)),
            dma((rhs,)),
            dma((rhs,)),
            dma((rhs,)),
            dma((rhs,)),
            dma((3, rhs // 2)),
            dma((3, rhs // 2)),
        ],
        compiler_params=pltpu.CompilerParams(
            collective_id=0, has_side_effects=True, vmem_limit_bytes=32 * 2**20
        ),
    )(*[pltpu.with_memory_space_constraint(x, pltpu.HBM) for x in operands])


def solution(mesh):
    return jax.shard_map(
        per_device,
        mesh=mesh,
        in_specs=(P(None, None, None, ("grp", "dev")), P(), P()),
        out_specs=P(None, None, None, ("grp", "dev")),
        check_vma=False,
    )
```
